32 devices in a mesh: section: 2 (over y), wide: 8 (over z, core), narrow: 2 (over x).
Axes of the slice: x: 2, y: 2, z: 4, core: 2. Of those that a mesh axis runs over, the one named last changes fastest.
Arguments:
- hidden: bfloat16 [2, 1024, 24576], P('section', None, 'wide'), may hold values from -6 to 6
- down_weight: bfloat16 [12288, 24576], P('narrow', 'wide'), may hold values from -0.0390625 to 0.0390625
- residual: bfloat16 [2, 1024, 12288], P('section', None, 'narrow'), may hold values from -6 to 6
- ln_gain: float32 [12288], P('narrow'), may hold values from 0.5 to 1.5
- ln_bias: float32 [12288], P('narrow'), may hold values from -3 to 3
- qkv_weight: bfloat16 [12288, 24576], P('narrow', 'wide'), may hold values from -1 to 1
Outputs:
- stream: bfloat16 [2, 1024, 12288], P('section', 'wide', 'narrow')
- context: bfloat16 [2, 1024, 8192], P('section', 'narrow', 'wide')
The draws below stay inside these ranges and needn't reach their ends.
All inputs are finite; a program needn't handle non-finite values.
Results may differ from the reference program's by a relative error of at most 0.007.
Values may be sent and summed in bfloat16 or wider, within the bound.
A program may use at most 320 MiB of HBM per device.

```python
import math
import jax
import jax.numpy as jnp
from jax import lax

D = 12288
FF = 24576
HEADS = 64
HDIM = 128
SEQ = 1024
N_SECTION = 2


def column_scale(low, high):
    ramp = jnp.arange(D, dtype=jnp.float32) / jnp.float32(max(D - 1, 1))
    return jnp.exp(jnp.float32(math.log(low)) + jnp.float32(math.log(high / low)) * ramp)


def draw_residual(key, part):
    fourth = jax.random.fold_in(jax.random.fold_in(key, 11), 3)
    result = jax.random.truncated_normal(fourth, -2.0, 2.0, (2, SEQ, D), jnp.float32) * column_scale(0.5, 3.0)[None, None, :]
    return result.astype(jnp.bfloat16)


def draw_qkv_weight(key, part):
    fourth = jax.random.fold_in(jax.random.fold_in(key, 23), 3)
    scale = jnp.float32(1.0 / math.sqrt(D))
    result = jax.random.truncated_normal(fourth, -6.0, 6.0, (D, 3 * HEADS * HDIM), jnp.float32) * scale
    return result.astype(jnp.bfloat16)


def with_spikes(array, own_key, source, target, blocks, factor):
    owner, partner = [(jnp.arange(array.shape[axis_at]) // (array.shape[axis_at] // blocks)).reshape([-1 if axis == axis_at else 1 for axis in range(array.ndim)]) for axis_at in (source, target)]
    chosen = jax.random.permutation(own_key, blocks)[partner]
    strong = (owner == chosen) | (owner == (partner + blocks // 2) % blocks)
    return jnp.where(strong, factor * array, array)


def steps_of(own_key, extent, cuts, smallest, largest):
    gain, own = 1.0, jax.random.fold_in(own_key, 6)
    for axis_at, shards_of in cuts:
        draws = jnp.exp(jax.random.uniform(jax.random.fold_in(own, axis_at), (shards_of,), jnp.float32, smallest / len(cuts), largest / len(cuts)))
        gain = gain * jnp.repeat(draws, extent[axis_at] // shards_of).reshape([-1 if axis == axis_at else 1 for axis in range(len(extent))])
    return gain


def centred(stream_key, dims, deviation, most, shards=(), held_as=jnp.bfloat16):
    factor_of = steps_of(stream_key, dims, shards, -0.22, 0.18) if shards else 1.0
    values = jax.random.normal(stream_key, dims, jnp.float32) * deviation * factor_of
    return jnp.minimum(jnp.maximum(values, -most), most).astype(held_as)


def noise_with(key, shape, spread, most, shards, heavy, kind=jnp.bfloat16):
    values = spread * jax.random.normal(key, shape, jnp.float32)
    if shards:
        values = values * steps_of(key, shape, shards, -0.22, 0.18)
    return jnp.clip(with_spikes(values, jax.random.fold_in(key, 3), *heavy), -most, most).astype(kind)


def setup_inputs(seed: int = 0) -> dict:
    streams_of = jax.random.split(jax.random.key(seed), 7)
    hidden = noise_with(streams_of[0], (N_SECTION, SEQ, FF), 1.0, 6.0, ((0, 2), (2, 8)), (2, 1, 8, 2.0))
    down_weight = centred(streams_of[1], (D, FF), FF ** -0.5, 0.0390625, ((0, 2), (1, 8)))
    residual = draw_residual(jax.random.fold_in(streams_of[6], 71), 0)
    ln_gain = jnp.clip(0.5 + 1.0 * jax.random.uniform(streams_of[3], (D,), jnp.float32) ** steps_of(streams_of[3], (D,), ((0, 2),), -0.2, 0.2), 0.5, 1.5)
    ln_bias = centred(streams_of[4], (D,), 0.5, 3.0, ((0, 2),), jnp.float32)
    qkv_weight = draw_qkv_weight(jax.random.fold_in(streams_of[6], 71), 0)
    return dict(hidden=hidden, down_weight=down_weight, residual=residual, ln_gain=ln_gain, ln_bias=ln_bias, qkv_weight=qkv_weight)


def attend(joined):
    parts = joined.reshape(SEQ, HEADS, 3, HDIM).astype(jnp.float32)
    query = parts[:, :, 0]
    keys = parts[:, :, 1]
    values = parts[:, :, 2]
    scores = jnp.einsum('qhd,khd->hqk', query, keys) / jnp.sqrt(jnp.float32(HDIM))
    rows = jnp.arange(SEQ)[:, None]
    cols = jnp.arange(SEQ)[None, :]
    scores = jnp.where((cols <= rows)[None], scores, jnp.float32(-1e+30))
    top = lax.optimization_barrier(jnp.max(scores, axis=2, keepdims=True))
    expd = jnp.exp(scores - top)
    probs = (expd / lax.optimization_barrier(jnp.sum(expd, axis=2, keepdims=True))).astype(jnp.bfloat16)
    out = jnp.einsum('hqk,khd->qhd', probs.astype(jnp.float32), values)
    return out.astype(jnp.bfloat16).reshape(SEQ, HEADS * HDIM)

def reference(hidden, down_weight, residual, ln_gain, ln_bias, qkv_weight):
    streams = []
    attended = []
    for micro in range(2):
        ffn = jnp.dot(hidden[micro], down_weight.T, preferred_element_type=jnp.float32)
        stream = (residual[micro].astype(jnp.float32) + ffn).astype(jnp.bfloat16)
        values = stream.astype(jnp.float32)
        mean = lax.optimization_barrier(jnp.sum(values, axis=1)) / D
        var = lax.optimization_barrier(jnp.sum(values * values, axis=1)) / D - mean * mean
        normed = ((values - mean[:, None]) * lax.rsqrt(var + 1e-05)[:, None] * ln_gain + ln_bias).astype(jnp.bfloat16)
        joined = jnp.dot(normed, qkv_weight, preferred_element_type=jnp.float32).astype(jnp.bfloat16)
        streams.append(stream)
        attended.append(attend(joined))
    return (jnp.stack(streams), jnp.stack([attended[1], attended[0]]))
```

```python
import functools

import jax
import jax.numpy as jnp
from jax import lax
from jax.experimental import pallas as pl
from jax.experimental.pallas import tpu as pltpu
from jax.sharding import PartitionSpec as P

D = 12288
HDIM = 128
CHUNKS = 2
QBLOCK = 256


def from_behind(value, axis, steps):
    count = lax.axis_size(axis)
    pairs = [(source, (source + steps) % count) for source in range(count)]
    return lax.ppermute(value, axis, pairs)


def attend_head(seq_len, joined_ref, out_ref):
    block = min(QBLOCK, seq_len)
    scale = 1.0 / (HDIM**0.5)
    for start in range(0, seq_len, block):
        stop = start + block
        query = joined_ref[start:stop, :HDIM]
        keys = joined_ref[:stop, HDIM : 2 * HDIM]
        vals = joined_ref[:stop, 2 * HDIM :]
        scores = (
            lax.dot_general(query, keys, (((1,), (1,)), ((), ())), preferred_element_type=jnp.float32)
            * scale
        )
        rows = start + lax.broadcasted_iota(jnp.int32, scores.shape, 0)
        cols = lax.broadcasted_iota(jnp.int32, scores.shape, 1)
        scores = jnp.where(cols <= rows, scores, jnp.float32(-1e30))
        top = jnp.max(scores, axis=1, keepdims=True)
        expd = jnp.exp(scores - top)
        probs = (expd * (1.0 / jnp.sum(expd, axis=1, keepdims=True))).astype(jnp.bfloat16)
        out_ref[start:stop, :] = jnp.dot(probs, vals, preferred_element_type=jnp.float32).astype(
            jnp.bfloat16
        )


def attention(joined):
    seq_len, width = joined.shape
    heads = width // (3 * HDIM)
    return pl.pallas_call(
        functools.partial(attend_head, seq_len),
        grid=(heads,),
        in_specs=[pl.BlockSpec((seq_len, 3 * HDIM), lambda h: (0, h))],
        out_specs=pl.BlockSpec((seq_len, HDIM), lambda h: (0, h)),
        out_shape=jax.ShapeDtypeStruct((seq_len, heads * HDIM), jnp.bfloat16),
        compiler_params=pltpu.CompilerParams(vmem_limit_bytes=32 << 20),
        cost_estimate=pl.CostEstimate(
            flops=3 * heads * seq_len * seq_len * HDIM,
            bytes_accessed=4 * 2 * seq_len * heads * HDIM,
            transcendentals=heads * seq_len * seq_len // 2,
        ),
    )(joined)


def split_heads(hidden, down_weight, residual, ln_gain, ln_bias, qkv_weight):
    inner = hidden[0]
    seq_len, units = inner.shape
    wide = lax.axis_size("wide")
    wide_rows = seq_len // wide
    part = wide_rows // CHUNKS
    wide_at = lax.axis_index("wide")
    narrow_at = lax.axis_index("narrow")
    half = qkv_weight.shape[1] // 2
    own_resid = lax.dynamic_slice_in_dim(residual[0], wide_at * wide_rows, wide_rows, 0)
    inner = inner.reshape(wide, CHUNKS, part, units)
    contract = (((1,), (1,)), ((), ()))
    streams, joins = [], []
    for chunk in range(CHUNKS):
        rows = inner[:, chunk].reshape(wide * part, units)
        partial_ffn = lax.dot_general(
            rows, down_weight, contract, preferred_element_type=jnp.float32
        ).astype(jnp.bfloat16)
        summed = lax.psum_scatter(partial_ffn, "wide", scatter_dimension=0, tiled=True)
        if chunk:
            summed, arrived = lax.optimization_barrier((summed, arrived))
        resid = own_resid[chunk * part : (chunk + 1) * part].astype(jnp.float32)
        mine = (resid + summed.astype(jnp.float32)).astype(jnp.bfloat16)
        streams.append(mine)
        values = mine.astype(jnp.float32)
        moments = jnp.stack([jnp.sum(values, axis=1), jnp.sum(values * values, axis=1)])
        totals, squares = moments + from_behind(moments, "narrow", 1)
        mean = totals / D
        var = squares / D - mean * mean
        normed = (
            (values - mean[:, None]) * lax.rsqrt(var + 1e-05)[:, None] * ln_gain + ln_bias
        ).astype(jnp.bfloat16)
        arrived = from_behind(normed, "section", 1)
        gathered = lax.all_gather(arrived, "wide", axis=0, tiled=True)
        partial_qkv = jnp.dot(gathered, qkv_weight, preferred_element_type=jnp.float32)
        other = lax.dynamic_slice_in_dim(partial_qkv, (1 - narrow_at) * half, half, 1)
        own = lax.dynamic_slice_in_dim(partial_qkv, narrow_at * half, half, 1)
        came = from_behind(other.astype(jnp.bfloat16), "narrow", 1)
        joined = (own + came.astype(jnp.float32)).astype(jnp.bfloat16)
        joins.append(joined.reshape(wide, part, half))
    own_rows = jnp.concatenate(streams, axis=0)
    joined = jnp.concatenate(joins, axis=1).reshape(seq_len, half)
    attended = attention(joined)
    query_count = seq_len // 2
    away = lax.dynamic_slice_in_dim(attended, (1 - narrow_at) * query_count, query_count, 0)
    home = lax.dynamic_slice_in_dim(attended, narrow_at * query_count, query_count, 0)
    came = from_behind(away, "narrow", 1)
    first = narrow_at == 0
    attended = jnp.concatenate(
        [jnp.where(first, home, came), jnp.where(first, came, home)], axis=1
    )
    return (own_rows[None], attended[None])


def split_queries(hidden, down_weight, residual, ln_gain, ln_bias, qkv_weight):
    inner = hidden[0]
    resid = residual[0]
    seq_len = inner.shape[0]
    wide_rows = seq_len // lax.axis_size("wide")
    wide_at = lax.axis_index("wide")
    contract = (((1,), (1,)), ((), ()))
    partial_ffn = lax.dot_general(inner, down_weight, contract, preferred_element_type=jnp.float32)
    summed = lax.psum(partial_ffn, "wide")
    mine = (resid.astype(jnp.float32) + summed).astype(jnp.bfloat16)
    arrived = from_behind(mine, "section", 1)
    own_rows = lax.dynamic_slice_in_dim(mine, wide_at * wide_rows, wide_rows, 0)
    values = arrived.astype(jnp.float32)
    totals, squares = lax.psum(
        (jnp.sum(values, axis=1), jnp.sum(values * values, axis=1)), "narrow"
    )
    mean = totals / D
    var = squares / D - mean * mean
    normed = (
        (values - mean[:, None]) * lax.rsqrt(var + 1e-05)[:, None] * ln_gain + ln_bias
    ).astype(jnp.bfloat16)
    heads_here = qkv_weight.shape[1] // (3 * HDIM)
    query_count = seq_len // lax.axis_size("narrow")
    narrow_at = lax.axis_index("narrow")
    joined = lax.psum(
        jnp.dot(normed, qkv_weight, preferred_element_type=jnp.float32), "narrow"
    ).astype(jnp.bfloat16)
    mine_joined = lax.dynamic_slice_in_dim(joined, narrow_at * query_count, query_count, 0)
    query = mine_joined.reshape(query_count, heads_here, 3, HDIM)[:, :, 0]
    pairs = joined.reshape(seq_len, heads_here, 3, HDIM)[:, :, 1:]
    keys = pairs[:, :, 0]
    vals = pairs[:, :, 1]
    scores = jnp.einsum("qhd,khd->hqk", query, keys, preferred_element_type=jnp.float32) / jnp.sqrt(
        jnp.float32(HDIM)
    )
    query_pos = narrow_at * query_count + lax.broadcasted_iota(jnp.int32, (query_count, seq_len), 0)
    key_pos = lax.broadcasted_iota(jnp.int32, (query_count, seq_len), 1)
    scores = jnp.where((key_pos <= query_pos)[None], scores, jnp.float32(-1e30))
    top = jnp.max(scores, axis=2, keepdims=True)
    expd = jnp.exp(scores - top)
    probs = (expd / jnp.sum(expd, axis=2, keepdims=True)).astype(jnp.bfloat16)
    attended = jnp.einsum("hqk,khd->qhd", probs, vals, preferred_element_type=jnp.float32).astype(
        jnp.bfloat16
    )
    attended = attended.reshape(query_count, heads_here * HDIM)
    return (own_rows[None], attended[None])


def per_device(hidden, down_weight, residual, ln_gain, ln_bias, qkv_weight):
    heads_here = qkv_weight.shape[1] // (3 * HDIM)
    wide_rows = hidden.shape[1] // lax.axis_size("wide")
    even = heads_here % 2 == 0 and wide_rows % (16 * CHUNKS) == 0
    plan = split_heads if lax.axis_size("narrow") == 2 and even else split_queries
    return plan(hidden, down_weight, residual, ln_gain, ln_bias, qkv_weight)


def solution(mesh):
    return jax.shard_map(
        per_device,
        mesh=mesh,
        in_specs=(
            P("section", None, "wide"),
            P("narrow", "wide"),
            P("section", None, "narrow"),
            P("narrow"),
            P("narrow"),
            P("narrow", "wide"),
        ),
        out_specs=(P("section", "wide", "narrow"), P("section", "narrow", "wide")),
        check_vma=False,
    )
```
